512 devices in a mesh: req: 128 (over y, z, core), tp: 4 (over x).
Axes of the slice: x: 4, y: 8, z: 8, core: 2. Of those that a mesh axis runs over, the one named last changes fastest.
Arguments:
- tokens: bfloat16 [16384, 1024], P('req'), may hold values from -6 to 6
- attn_heads: bfloat16 [16384, 1024], P('req', 'tp'), may hold values from -6 to 6
- out_proj: bfloat16 [1024, 1024], P('tp'), may hold values from -0.1875 to 0.1875
- norm_gain: float32 [1024], replicated, may hold values from 0.3 to 1.7
- w_gate: bfloat16 [32, 1024, 512], P(None, 'req', 'tp'), may hold values from -0.1875 to 0.1875
- w_up: bfloat16 [32, 1024, 512], P(None, 'req', 'tp'), may hold values from -0.1875 to 0.1875
- w_down: bfloat16 [32, 1024, 512], P(None, 'req', 'tp'), may hold values from -0.25 to 0.25
- routes: int32 [16384, 8], P('req'), may hold values from 0 to 31, all different within a row; in each aligned block of 32 rows (0 to 31, 32 to 63, ...) at most 12 rows name the same one
- gate_weights: float32 [16384, 8], P('req'), may hold values from 0.05 to 0.45
- cache_pages: bfloat16 [1024, 128, 8, 128], P('req', None, 'tp'), may hold values from -6 to 6
- page_dest: int32 [1024], P('req'), may hold values from 0 to 1023, as said below
Outputs:
- layer_output: bfloat16 [16384, 1024], P('req', 'tp')
- decode_cache: bfloat16 [1024, 128, 8, 128], P('req', None, 'tp')
The draws below stay inside these ranges and needn't reach their ends.
Inputs may be any that keep to these rules, and one draw needn't show every extreme that they name: `routes`: within each aligned block of 32 rows no expert is named by more than 12 rows, and some block reaches 12. The page p of index r of req (p among its 8 pages) is sent to the index r + k modulo 128 for some k from 0 to 7, into its decode slot k: page_dest[p] = ((r + k) % 128) * 8 + k. The 8 pages of one index use each k once, so every decode slot gets one page.
All inputs are finite; a program needn't handle non-finite values.
Results may differ from the reference program's by a relative error of at most 0.012.
Values may be sent and summed in bfloat16 or wider, within the bound.
A program may use at most 64 MiB of HBM per device.

```python
import math
import jax
import jax.numpy as jnp
import numpy as np
from jax import lax

D = 1024
FF = 512
EXPERTS = 32
TOP = 8
HEADS = 16
KVH = 8
HD = 64
PAGE = 128
SPREAD = 8
TOKENS = 16384
BLOCK = 32
CAP = 12
PAGES = 1024
N_REQ = 128
N_TP = 4


def draw_page_dest(key, part):
    row_keys = jax.random.split(jax.random.fold_in(key, 17), N_REQ)
    orders = jax.vmap(lambda single: jax.random.permutation(single, SPREAD))(row_keys).astype(jnp.int32)
    sources = jnp.arange(N_REQ, dtype=jnp.int32)[:, None]
    targets = (sources + orders) % N_REQ * SPREAD + orders
    return targets.reshape(-1).astype(jnp.int32)


def block_scale(own_key, dims, shards, low, largest):
    def one(axis_at, parts):
        steps = jax.random.uniform(jax.random.fold_in(jax.random.fold_in(own_key, 6), axis_at), (parts,), jnp.float32, low / len(shards), largest / len(shards))
        return jnp.repeat(jnp.exp(steps), dims[axis_at] // parts).reshape((-1,) + (1,) * (len(dims) - axis_at - 1))

    level = one(*shards[0])
    for cut in shards[1:]:
        level = level * one(*cut)
    return level


def shared_out(own_key, own, number, rows, number_of, top, most, skew):
    sequence = jax.random.permutation(own_key, number_of)
    crowded, usual = shares(number_of, rows * top, most, skew, True), shares(number_of, rows * top, most, skew, False)
    places = jnp.arange(number_of)

    def named(tallies, rotation):
        used = int((tallies > 0).sum())
        fixed = max(1, used // 4)
        shifted = fixed + (places - fixed + rotation * (used - fixed)) % max(1, number_of - fixed)
        return jnp.zeros((number_of,), jnp.int32).at[sequence[jnp.where(places < fixed, places, shifted)]].set(jnp.asarray(tallies, jnp.int32))

    tallies = jnp.where(number % 4 == 0, named(crowded, number // 4), named(usual, number - number // 4 - 1))
    mixed = jax.random.permutation(jax.random.fold_in(own, 3), number_of)
    giver, receiver = mixed[0:number_of // 2 * 2:2], mixed[1:number_of // 2 * 2:2]
    room = jnp.minimum(tallies[giver] - 1, most - tallies[receiver]) // 2
    room = jnp.where((giver == sequence[0]) | (receiver == sequence[0]) | (tallies[receiver] == 0), 0, jnp.maximum(room, 0))
    shifted = jax.random.randint(jax.random.fold_in(own, 4), (number_of // 2,), 0, 1 << 20) % (room + 1)
    tallies = tallies.at[giver].add(-shifted).at[receiver].add(shifted)
    members = jnp.searchsorted(jnp.cumsum(tallies), jnp.arange(rows * top), side="right").astype(jnp.int32)
    grid = members.reshape(top, rows).T
    grid = grid[jax.random.permutation(jax.random.fold_in(own, 1), rows)]
    rotation = jax.random.randint(jax.random.fold_in(own, 2), (rows, 1), 0, top)
    return jnp.take_along_axis(grid, (jnp.arange(top)[None, :] + rotation) % top, axis=1)


def shares(count, total, most, skew, full):
    weights = [(1 << 20) // math.isqrt(rank ** skew) + 1 for rank in range(1, count + 1)]
    largest = most if full else min(most, max(-(-total // count), total * weights[0] // sum(weights)))
    least = 1 if total - largest >= count - 1 else 0
    counts, spare = [largest] + [least] * (count - 1), total - largest - least * (count - 1)
    while spare > 0:
        free = [i for i in range(1, count) if counts[i] < largest] or [i for i in range(1, count) if counts[i] < most]
        whole, remaining = sum([weights[i] for i in free]), spare
        for i in free:
            extra = min(most - counts[i], max(1, remaining * weights[i] // whole), spare)
            counts[i] = counts[i] + extra
            spare = spare - extra
    return np.array(counts)


def noise(own_key, dims, spread, limit, cuts=(), kind=jnp.bfloat16):
    array = jax.random.normal(own_key, dims, jnp.float32) * spread
    if len(cuts) > 0:
        array = block_scale(own_key, dims, cuts, -0.22, 0.18) * array
    return jnp.clip(array, min=-limit, max=limit).astype(kind)


def setup_inputs(seed: int = 0) -> dict:
    splits = jax.random.split(jax.random.key(seed), 12)
    tokens = noise(splits[0], (TOKENS, D), 1.0, 6.0, ((0, 128),))
    attn_heads = noise(splits[1], (TOKENS, HEADS * HD), 1.0, 6.0, ((0, 128), (1, 4)))
    out_proj = noise(splits[2], (HEADS * HD, D), (HEADS * HD) ** -0.5, 0.1875, ((0, 4),))
    norm_gain = jnp.clip(jax.random.uniform(splits[3], (D,), jnp.float32, 0.3, 1.7), 0.3, 1.7)
    w_gate = noise(splits[4], (EXPERTS, D, FF), D ** -0.5, 0.1875, ((1, 128), (2, 4)))
    w_up = noise(splits[5], (EXPERTS, D, FF), D ** -0.5, 0.1875, ((1, 128), (2, 4)))
    w_down = noise(splits[6], (EXPERTS, D, FF), FF ** -0.5, 0.25, ((1, 128), (2, 4)))
    routes_keys = jax.random.split(jax.random.fold_in(splits[7], 1), TOKENS // BLOCK)
    routes_turns = jax.random.permutation(jax.random.fold_in(splits[7], 3), TOKENS // BLOCK)
    routes = jax.vmap(lambda own, number: shared_out(jax.random.fold_in(splits[7], 2), own, number, BLOCK, EXPERTS, TOP, CAP, 1))(routes_keys, routes_turns).reshape((TOKENS, TOP))
    gate_weights = jnp.clip(0.05 + 0.39999999 * jax.random.uniform(splits[8], (TOKENS, TOP), jnp.float32) ** block_scale(splits[8], (TOKENS, TOP), ((0, 128),), -0.2, 0.2), 0.05, 0.45)
    cache_pages = noise(splits[9], (PAGES, PAGE, KVH, 2 * HD), 1.0, 6.0, ((0, 128), (2, 4)))
    page_dest = draw_page_dest(jax.random.fold_in(splits[11], 71), 0)
    return dict(tokens=tokens, attn_heads=attn_heads, out_proj=out_proj, norm_gain=norm_gain, w_gate=w_gate, w_up=w_up, w_down=w_down, routes=routes, gate_weights=gate_weights, cache_pages=cache_pages, page_dest=page_dest)


def reference(tokens, attn_heads, out_proj, norm_gain, w_gate, w_up, w_down, routes, gate_weights, cache_pages, page_dest):
    attention = jnp.dot(attn_heads, out_proj, preferred_element_type=jnp.float32)
    residual = tokens.astype(jnp.float32) + attention
    inverse = lax.rsqrt(lax.optimization_barrier(jnp.mean(residual * residual, axis=1, keepdims=True)) + 1e-05)
    normed = (residual * inverse * norm_gain).astype(jnp.bfloat16)
    routed = routes.reshape(-1)
    weighting = gate_weights.reshape(-1)
    row_bound = TOKENS // BLOCK * CAP
    group_width = FF // N_TP
    positions = jnp.arange(row_bound, dtype=jnp.int32)

    def one_expert(mixture, expert):
        chosen = routed == expert
        picked = jnp.nonzero(chosen, size=row_bound, fill_value=0)[0].astype(jnp.int32)
        live_rows = positions < jnp.sum(chosen.astype(jnp.int32))
        owners = picked // TOP
        inputs = normed[owners]
        gate_mat = lax.dynamic_index_in_dim(w_gate, expert, 0, keepdims=False)
        up_mat = lax.dynamic_index_in_dim(w_up, expert, 0, keepdims=False)
        down_mat = lax.dynamic_index_in_dim(w_down, expert, 0, keepdims=False)
        pre_gate = jnp.dot(inputs, gate_mat, preferred_element_type=jnp.float32)
        pre_up = jnp.dot(inputs, up_mat, preferred_element_type=jnp.float32)
        active = (jax.nn.silu(pre_gate) * pre_up).astype(jnp.bfloat16)
        summed = jnp.zeros((row_bound, D), jnp.float32)
        for group_index in range(N_TP):
            group_start = group_index * group_width
            portion = lax.dot_general(active[:, group_start:group_start + group_width], down_mat[:, group_start:group_start + group_width], (((1,), (1,)), ((), ())), preferred_element_type=jnp.float32)
            rounded = lax.optimization_barrier(portion.astype(jnp.bfloat16))
            summed = summed + rounded.astype(jnp.float32)
        factor = jnp.where(live_rows, weighting[picked], jnp.zeros((), jnp.float32))
        mixture = mixture.at[owners].add(factor[:, None] * summed)
        return (mixture, None)
    mixture, unused = lax.scan(one_expert, jnp.zeros((TOKENS, D), jnp.float32), jnp.arange(EXPERTS, dtype=jnp.int32))
    layer_output = (residual + mixture).astype(jnp.bfloat16)
    decode_cache = jnp.zeros_like(cache_pages).at[page_dest].set(cache_pages)
    return (layer_output, decode_cache)
```

```python
import jax
import jax.numpy as jnp
import numpy as np
from jax import lax
from jax.sharding import PartitionSpec as P


def passed_along(value, axis, steps):
    count = lax.axis_size(axis)
    pairs = [(source, (source + steps) % count) for source in range(count)]
    return lax.ppermute(value, axis, pairs)


def gathered_weight(weight):
    experts, rows, hidden = weight.shape
    flat = jnp.transpose(weight, (1, 0, 2)).reshape(rows, experts * hidden)
    return lax.all_gather(flat, "req", axis=0, tiled=True)


def on_device(
    tokens,
    attn_heads,
    out_proj,
    norm_gain,
    w_gate,
    w_up,
    w_down,
    routes,
    gate_weights,
    cache_pages,
    page_dest,
):
    tp_count = lax.axis_size("tp")
    tp_place = lax.axis_index("tp")
    tok_count, top_count = routes.shape
    experts, _, hidden = w_gate.shape
    model_width = tokens.shape[1]
    quarter_rows = tok_count // tp_count

    gate_full = gathered_weight(w_gate)
    up_full = gathered_weight(w_up)
    down_full = gathered_weight(w_down)

    partial_value = jnp.dot(attn_heads, out_proj, preferred_element_type=jnp.float32)
    partial_sent = partial_value.astype(jnp.bfloat16)

    def rows_of(value, block):
        return lax.dynamic_slice_in_dim(value, block * quarter_rows, quarter_rows, 0)

    attention = rows_of(partial_value, tp_place)
    for step in range(1, tp_count):
        outgoing = rows_of(partial_sent, (tp_place + step) % tp_count)
        attention = attention + passed_along(outgoing, "tp", step).astype(jnp.float32)
    residual = rows_of(tokens, tp_place).astype(jnp.float32) + attention
    inverse = lax.rsqrt(jnp.mean(residual * residual, axis=1, keepdims=True) + 1e-05)
    normed_own = (residual * inverse * norm_gain).astype(jnp.bfloat16)
    normed = jnp.zeros((tok_count, model_width), jnp.bfloat16)
    normed = lax.dynamic_update_slice_in_dim(normed, normed_own, tp_place * quarter_rows, 0)
    for step in range(1, tp_count):
        block = (tp_place - step) % tp_count
        normed = lax.dynamic_update_slice_in_dim(
            normed, passed_along(normed_own, "tp", step), block * quarter_rows, 0
        )

    expert_ids = jnp.arange(experts, dtype=jnp.int32)
    factor = jnp.sum(
        jnp.where(routes[:, :, None] == expert_ids, gate_weights[:, :, None], 0.0), axis=1
    )
    factor_wide = jnp.broadcast_to(
        factor[:, :, None], (tok_count, experts, hidden)
    ).reshape(tok_count, experts * hidden)

    pre_gate = jnp.dot(normed, gate_full, preferred_element_type=jnp.float32)
    pre_up = jnp.dot(normed, up_full, preferred_element_type=jnp.float32)
    active = (factor_wide * (jax.nn.silu(pre_gate) * pre_up)).astype(jnp.bfloat16)
    combined = lax.dot_general(
        active, down_full, (((1,), (1,)), ((), ())), preferred_element_type=jnp.float32
    )
    own_rows = rows_of(combined, tp_place) + residual
    combined = lax.dynamic_update_slice_in_dim(combined, own_rows, tp_place * quarter_rows, 0)
    layer_output = lax.psum_scatter(
        combined.astype(jnp.bfloat16), "tp", scatter_dimension=1, tiled=True
    )

    spread = cache_pages.shape[0]
    page_offsets = page_dest % spread
    page_order = (
        jnp.zeros((spread,), jnp.int32).at[page_offsets].set(jnp.arange(spread, dtype=jnp.int32))
    )
    ranked = cache_pages[page_order]
    arrived_pages = [ranked[0]]
    for offset in range(1, spread):
        arrived_pages.append(passed_along(ranked[offset], "req", offset))
    decode_cache = jnp.stack(arrived_pages)
    return (layer_output, decode_cache)


def solution(mesh):
    in_specs = (
        P("req", None),
        P("req", "tp"),
        P("tp", None),
        P(),
        P(None, "req", "tp"),
        P(None, "req", "tp"),
        P(None, "req", "tp"),
        P("req", None),
        P("req", None),
        P("req", None, "tp", None),
        P("req"),
    )
    out_specs = (P("req", "tp"), P("req", None, "tp", None))
    return jax.shard_map(
        on_device, mesh=mesh, in_specs=in_specs, out_specs=out_specs, check_vma=False
    )
```

```python
import functools

import jax
import jax.numpy as jnp
from jax import lax
from jax.experimental import pallas as pl
from jax.experimental.pallas import tpu as pltpu
from jax.sharding import PartitionSpec as P

MESH = pl.DeviceIdType.MESH
RING = 8
CORES = 2
STREAMS = 4
LAST = RING - 1
F32 = jnp.float32
BF16 = jnp.bfloat16


def expert_kernel(
    req_count,
    tp_count,
    part_ref,
    tokens_ref,
    factor_ref,
    gain_ref,
    gate_ref,
    up_ref,
    down_ref,
    pages_ref,
    out_ref,
    cache_ref,
    full,
    parts,
    both,
    factors,
    normed,
    residual,
    active,
    outbox,
    inbox,
    local_sem,
    swap_sem,
    part_sem,
    page_sem,
    first_sem,
    second_sem,
    back_sem,
):
    peers = tp_count * CORES
    me = lax.axis_index("req")
    tp = lax.axis_index("tp")
    core = lax.rem(me, CORES)
    z = lax.rem(me // CORES, RING)
    y = me // (CORES * RING)
    mine = tp * CORES + core
    other = 1 - core
    chip = me - core
    tok_count, width = tokens_ref.shape
    half = full.shape[4]
    cut = half // STREAMS
    pages = pages_ref.shape[0]
    share = width // tp_count

    def at(y_place, z_place, core_place):
        return (y_place * RING + z_place) * CORES + core_place

    def peer(index):
        return (chip + lax.rem(index, CORES), index // CORES)

    ahead_y = (at(lax.rem(y + 1, RING), z, core), tp)
    behind_y = (at(lax.rem(y + LAST, RING), z, core), tp)
    ahead_z = (at(y, lax.rem(z + 1, RING), core), tp)
    behind_z = (at(y, lax.rem(z + LAST, RING), core), tp)
    partner = (chip + other, tp)

    barrier = pltpu.get_barrier_semaphore()

    def greet(device):
        pl.semaphore_signal(barrier, inc=1, device_id=device, device_id_type=MESH)

    for device in (ahead_y, behind_y, ahead_z, behind_z):
        greet(device)
    for step in range(1, peers):
        greet(peer(lax.rem(mine + step, peers)))
    for step in range(1, pages):
        greet((lax.rem(me + step, req_count), tp))
        greet((lax.rem(me + req_count - step, req_count), tp))
    pl.semaphore_wait(barrier, 4 + peers - 1 + 2 * (pages - 1))

    def remote(source, target, sems, device):
        return pltpu.make_async_remote_copy(
            src_ref=source,
            dst_ref=target,
            send_sem=sems.at[0],
            recv_sem=sems.at[1],
            device_id=device,
            device_id_type=MESH,
        )

    rows = pl.ds(pl.multiple_of(core * 8, 8), 8)
    kept = pl.ds(pl.multiple_of(core * half, half), half)
    given = pl.ds(pl.multiple_of(other * half, half), half)
    swaps, locals_ = [], []
    for index, weight in enumerate((gate_ref, up_ref, down_ref)):
        place = full.at[index, y, z, rows, :]
        swaps.append(remote(weight.at[:, given], place, swap_sem.at[index], partner))
        locals_.append(pltpu.make_async_copy(weight.at[:, kept], place, local_sem.at[index]))
    swaps.append(remote(tokens_ref, both.at[core], swap_sem.at[3], partner))
    swaps.append(remote(factor_ref.at[other], factors.at[core], swap_sem.at[4], partner))
    locals_.append(pltpu.make_async_copy(tokens_ref, both.at[core], local_sem.at[3]))
    locals_.append(pltpu.make_async_copy(factor_ref.at[core], factors.at[core], local_sem.at[4]))
    locals_.append(pltpu.make_async_copy(part_ref, parts.at[mine], local_sem.at[5]))
    locals_.append(pltpu.make_async_copy(pages_ref.at[0], cache_ref.at[0], local_sem.at[6]))
    for copy in swaps + locals_:
        copy.start()

    def page_copy(step):
        device = (lax.rem(me + step, req_count), tp)
        return remote(pages_ref.at[step], cache_ref.at[step], page_sem.at[step], device)

    def part_copy(step):
        device = peer(lax.rem(mine + step, peers))
        return remote(part_ref, parts.at[mine], part_sem.at[step], device)

    for step in range(1, peers):
        part_copy(step).start()
    for step in range(pages - 1, 0, -1):
        page_copy(step).start()
    for index in range(3):
        swaps[index].wait_recv()
        locals_[index].wait()

    def back(place, step):
        return lax.rem(place + RING - step, RING)

    def forth(place, step):
        return lax.rem(place + step, RING)

    def first_copy(stream, step):
        columns = pl.ds(stream * cut, cut)
        y_place, z_place = (
            (back(y, step), z),
            (forth(y, step), z),
            (y, back(z, step)),
            (y, forth(z, step)),
        )[stream]
        device = (ahead_y, behind_y, ahead_z, behind_z)[stream]
        block = full.at[:, y_place, z_place, :, columns]
        return remote(block, block, first_sem.at[stream, step], device)

    def second_copy(piece, stream, step):
        weight = min(piece, 2)
        size = cut if piece < 2 else cut // 2
        columns = pl.ds(stream * cut + max(piece - 2, 0) * size, size)
        device = (ahead_z, behind_z, ahead_y, behind_y)[stream]
        if stream == 0:
            block = full.at[weight, :, back(z, step), :, columns]
        elif stream == 1:
            block = full.at[weight, :, forth(z, step), :, columns]
        elif stream == 2:
            block = full.at[weight, back(y, step), :, :, columns]
        else:
            block = full.at[weight, forth(y, step), :, :, columns]
        return remote(block, block, second_sem.at[piece, stream, step], device)

    def first_step(step, carry):
        for stream in range(STREAMS):
            first_copy(stream, step).start()
        for stream in range(STREAMS):
            first_copy(stream, step).wait_recv()
        return carry

    lax.fori_loop(0, LAST, first_step, 0)

    for piece in (0, 1):
        for stream in range(STREAMS):
            second_copy(piece, stream, 0).start()

    def second_step(pieces, step):
        for piece in pieces:
            for stream in range(STREAMS):
                second_copy(piece, stream, step - 1).wait_recv()
                second_copy(piece, stream, step).start()

    second_step((0, 1), 1)

    for step in range(1, peers):
        part_copy(step).wait_recv()
    for index in (3, 4):
        swaps[index].wait_recv()
    for index in (3, 4, 5):
        locals_[index].wait()
    lines = 32

    def norm_step(step, carry):
        which = step // (tok_count // lines)
        start = pl.multiple_of(lax.rem(step, tok_count // lines) * lines, lines)
        span = pl.ds(start, lines)
        total = both[which, span, :].astype(F32)
        for place in range(tp_count):
            total = total + parts[place * CORES + which, span, :].astype(F32)
        residual[which, span, :] = total
        inverse = lax.rsqrt(jnp.mean(total * total, axis=1, keepdims=True) + 1e-05)
        normed[which, span, :] = (total * inverse * gain_ref[...]).astype(BF16)
        return carry

    lax.fori_loop(0, CORES * tok_count // lines, norm_step, 0)

    def gate_up_step(step, carry):
        second_step((0, 1), step)
        return carry

    lax.fori_loop(2, LAST, gate_up_step, 0)
    for piece in (2, 3):
        for stream in range(STREAMS):
            second_copy(piece, stream, 0).start()
    for piece in (0, 1):
        for stream in range(STREAMS):
            second_copy(piece, stream, LAST - 1).wait_recv()

    chunk = half // RING
    hidden = 128
    all_rows = CORES * tok_count

    def expert_part(index):
        columns = pl.ds(pl.multiple_of(index * chunk, chunk), chunk)
        lhs = normed[...].reshape(all_rows, width)
        pre_gate = jnp.dot(
            lhs, full[0, :, :, :, columns].reshape(width, chunk), preferred_element_type=F32
        )
        pre_up = jnp.dot(
            lhs, full[1, :, :, :, columns].reshape(width, chunk), preferred_element_type=F32
        )
        value = pre_gate / (1.0 + jnp.exp(-pre_gate)) * pre_up
        table = factors[...].reshape(all_rows, 128)
        lanes = lax.broadcasted_iota(jnp.int32, table.shape, 1)
        for expert in range(chunk // hidden):
            picked = jnp.where(lanes == index * (chunk // hidden) + expert, table, 0.0)
            weight = jnp.sum(picked, axis=1, keepdims=True)
            scaled = value[:, expert * hidden : (expert + 1) * hidden] * weight
            spot = pl.ds(pl.multiple_of(index * chunk + expert * hidden, hidden), hidden)
            active[:, spot] = scaled.astype(BF16)

    expert_part(0)

    def down_step(step, carry):
        second_step((2, 3), step)
        expert_part(step)
        return carry

    lax.fori_loop(1, LAST, down_step, 0)
    expert_part(LAST)
    for piece in (2, 3):
        for stream in range(STREAMS):
            second_copy(piece, stream, LAST - 1).wait_recv()

    def back_copy(place, which):
        index = place * CORES + which
        step = lax.rem(index + peers - mine, peers)
        return remote(
            outbox.at[place, which],
            inbox.at[mine],
            back_sem.at[step],
            (chip + which, place),
        )

    height = RING // tp_count

    def down_part(place):
        block = full[2, pl.ds(place * height, height)].reshape(share, half)
        return lax.dot_general(
            active[...], block, (((1,), (1,)), ((), ())), preferred_element_type=F32
        )

    def down_turn(step, carry):
        place = lax.rem(tp + step, tp_count)
        value = down_part(place)
        outbox[place] = value.astype(BF16).reshape(CORES, tok_count, share)
        return carry

    for step in range(1, tp_count):
        down_turn(step, 0)
        if step > 1:
            place = lax.rem(tp + step - 1, tp_count)
            for which in range(CORES):
                back_copy(place, which).start()
    down_turn(0, 0)
    place = lax.rem(tp + tp_count - 1, tp_count)
    for which in range(CORES):
        back_copy(place, which).start()
    back_copy(tp, other).start()

    columns = pl.ds(pl.multiple_of(tp * share, share), share)
    total = residual[core, :, columns] + outbox[tp, core].astype(F32)

    def came(step):
        return remote(outbox.at[tp, other], inbox.at[mine], back_sem.at[step], partner)

    for step in range(1, peers):
        came(step).wait_recv()
        source = lax.rem(mine + peers - step, peers)
        total = total + inbox[source].astype(F32)
    out_ref[...] = total.astype(out_ref.dtype)

    for step in range(1, peers):
        came(step).wait_send()
        part_copy(step).wait_send()
    for copy in swaps:
        copy.wait_send()
    locals_[6].wait()
    for step in range(1, pages):
        page_copy(step).wait()

    def drain(step, carry):
        for stream in range(STREAMS):
            first_copy(stream, step).wait_send()
            for piece in range(4):
                second_copy(piece, stream, step).wait_send()
        return carry

    lax.fori_loop(0, LAST, drain, 0)


def on_device(
    tokens,
    attn_heads,
    out_proj,
    norm_gain,
    w_gate,
    w_up,
    w_down,
    routes,
    gate_weights,
    cache_pages,
    page_dest,
):
    req_count = lax.axis_size("req")
    tp_count = lax.axis_size("tp")
    tok_count, top_count = routes.shape
    experts, rows, hidden = w_gate.shape
    width = tokens.shape[1]
    half = experts * hidden // CORES

    def flat(weight):
        return jnp.transpose(weight, (1, 0, 2)).reshape(rows, experts * hidden)

    part = jnp.dot(attn_heads, out_proj, preferred_element_type=F32).astype(BF16)

    lanes = jnp.arange(128, dtype=jnp.int32)
    own = experts // CORES
    ids = jnp.stack([jnp.where(lanes < own, lanes + h * own, -1) for h in range(CORES)])
    factor = jnp.zeros((CORES, tok_count, 128), F32)
    for route in range(top_count):
        factor = factor + jnp.where(
            routes[None, :, route, None] == ids[:, None, :], gate_weights[None, :, route, None], 0.0
        )

    spread = cache_pages.shape[0]
    places = jnp.arange(spread, dtype=jnp.int32)
    page_order = jnp.sum(
        jnp.where((page_dest % spread)[None, :] == places[:, None], places[None, :], 0), axis=1
    )
    ranked = cache_pages[page_order]

    vmem = pl.BlockSpec(memory_space=pltpu.VMEM)
    anywhere = pl.BlockSpec(memory_space=pl.ANY)
    peers = tp_count * CORES
    share = width // tp_count
    dma = pltpu.SemaphoreType.DMA
    return pl.pallas_call(
        functools.partial(expert_kernel, req_count, tp_count),
        out_shape=(
            jax.ShapeDtypeStruct((tok_count, share), BF16),
            jax.ShapeDtypeStruct(cache_pages.shape, BF16),
        ),
        in_specs=[vmem] * 7 + [anywhere],
        out_specs=(vmem, anywhere),
        scratch_shapes=[
            pltpu.VMEM((3, RING, RING, CORES * rows, half), BF16),
            pltpu.VMEM((peers, tok_count, width), BF16),
            pltpu.VMEM((CORES, tok_count, width), BF16),
            pltpu.VMEM((CORES, tok_count, 128), F32),
            pltpu.VMEM((CORES, tok_count, width), BF16),
            pltpu.VMEM((CORES, tok_count, width), F32),
            pltpu.VMEM((CORES * tok_count, half), BF16),
            pltpu.VMEM((tp_count, CORES, tok_count, share), BF16),
            pltpu.VMEM((peers, tok_count, share), BF16),
            dma((7,)),
            dma((5, 2)),
            dma((peers, 2)),
            dma((spread, 2)),
            dma((STREAMS, LAST, 2)),
            dma((4, STREAMS, LAST, 2)),
            dma((peers, 2)),
        ],
        compiler_params=pltpu.CompilerParams(
            collective_id=0, has_side_effects=True, vmem_limit_bytes=48 * 1024 * 1024
        ),
    )(part, tokens, factor, norm_gain[None, :], flat(w_gate), flat(w_up), flat(w_down), ranked)


def solution(mesh):
    in_specs = (
        P("req", None),
        P("req", "tp"),
        P("tp", None),
        P(),
        P(None, "req", "tp"),
        P(None, "req", "tp"),
        P(None, "req", "tp"),
        P("req", None),
        P("req", None),
        P("req", None, "tp", None),
        P("req"),
    )
    out_specs = (P("req", "tp"), P("req", None, "tp", None))
    return jax.shard_map(
        on_device, mesh=mesh, in_specs=in_specs, out_specs=out_specs, check_vma=False
    )
```

```python
import functools

import jax
import jax.numpy as jnp
from jax import lax
from jax.experimental import pallas as pl
from jax.experimental.pallas import tpu as pltpu
from jax.sharding import PartitionSpec as P

MESH = pl.DeviceIdType.MESH
RING = 8
CORES = 2
STREAMS = 4
LAST = RING - 1
HOPS = ((4, 3), (3, 4))
TILES = ((2, 5, 5, 4), (3, 4, 4, 5), (4, 4, 4, 4))
F32 = jnp.float32
BF16 = jnp.bfloat16


def expert_kernel(
    req_count,
    tp_count,
    part_ref,
    tokens_ref,
    factor_ref,
    gain_ref,
    gate_ref,
    up_ref,
    down_ref,
    pages_ref,
    out_ref,
    cache_ref,
    full,
    parts,
    both,
    factors,
    normed,
    residual,
    active,
    outbox,
    inbox,
    local_sem,
    swap_sem,
    part_sem,
    page_sem,
    first_sem,
    second_sem,
    back_sem,
):
    peers = tp_count * CORES
    me = lax.axis_index("req")
    tp = lax.axis_index("tp")
    core = lax.rem(me, CORES)
    z = lax.rem(me // CORES, RING)
    y = me // (CORES * RING)
    mine = tp * CORES + core
    other = 1 - core
    chip = me - core
    tok_count, width = tokens_ref.shape
    half = full.shape[4]
    pages = pages_ref.shape[0]
    share = width // tp_count

    def at(y_place, z_place, core_place):
        return (y_place * RING + z_place) * CORES + core_place

    def peer(index):
        return (chip + lax.rem(index, CORES), index // CORES)

    ahead_y = (at(lax.rem(y + 1, RING), z, core), tp)
    behind_y = (at(lax.rem(y + LAST, RING), z, core), tp)
    ahead_z = (at(y, lax.rem(z + 1, RING), core), tp)
    behind_z = (at(y, lax.rem(z + LAST, RING), core), tp)
    partner = (chip + other, tp)

    barrier = pltpu.get_barrier_semaphore()

    def greet(device):
        pl.semaphore_signal(barrier, inc=1, device_id=device, device_id_type=MESH)

    for device in (ahead_y, behind_y, ahead_z, behind_z):
        greet(device)
    for step in range(1, peers):
        greet(peer(lax.rem(mine + step, peers)))
    for step in range(1, pages):
        greet((lax.rem(me + step, req_count), tp))
        greet((lax.rem(me + req_count - step, req_count), tp))
    pl.semaphore_wait(barrier, 4 + peers - 1 + 2 * (pages - 1))

    def remote(source, target, sems, device):
        return pltpu.make_async_remote_copy(
            src_ref=source,
            dst_ref=target,
            send_sem=sems.at[0],
            recv_sem=sems.at[1],
            device_id=device,
            device_id_type=MESH,
        )

    rows = pl.ds(pl.multiple_of(core * 8, 8), 8)
    kept = pl.ds(pl.multiple_of(core * half, half), half)
    given = pl.ds(pl.multiple_of(other * half, half), half)
    swaps, locals_ = [], []
    for index, weight in enumerate((gate_ref, up_ref, down_ref)):
        place = full.at[index, y, z, rows, :]
        swaps.append(remote(weight.at[:, given], place, swap_sem.at[index], partner))
        locals_.append(pltpu.make_async_copy(weight.at[:, kept], place, local_sem.at[index]))
    swaps.append(remote(tokens_ref, both.at[core], swap_sem.at[3], partner))
    swaps.append(remote(factor_ref.at[other], factors.at[core], swap_sem.at[4], partner))
    locals_.append(pltpu.make_async_copy(tokens_ref, both.at[core], local_sem.at[3]))
    locals_.append(pltpu.make_async_copy(factor_ref.at[core], factors.at[core], local_sem.at[4]))
    locals_.append(pltpu.make_async_copy(part_ref, parts.at[mine], local_sem.at[5]))
    locals_.append(pltpu.make_async_copy(pages_ref.at[0], cache_ref.at[0], local_sem.at[6]))
    for copy in swaps + locals_:
        copy.start()

    def page_copy(step):
        device = (lax.rem(me + step, req_count), tp)
        return remote(pages_ref.at[step], cache_ref.at[step], page_sem.at[step], device)

    def part_copy(step):
        device = peer(lax.rem(mine + step, peers))
        return remote(part_ref, parts.at[mine], part_sem.at[step], device)

    for index in range(3):
        swaps[index].wait_recv()
        locals_[index].wait()

    def back(place, step):
        return lax.rem(place + RING - step, RING)

    def forth(place, step):
        return lax.rem(place + step, RING)

    def span_of(weight, first, last):
        start = sum(TILES[weight][:first]) * 128
        return pl.ds(start, sum(TILES[weight][first:last]) * 128)

    along = ((ahead_y, behind_y), (ahead_z, behind_z))

    def place_of(axis, sign, step):
        return (back, forth)[sign]((y, z)[axis], step)

    def first_copy(axis, sign, part, step):
        weights = (pl.ds(0, 2), pl.ds(2, 1))[part]
        columns = span_of(2 * part, 2 * axis, 2 * axis + 2)
        place = place_of(axis, sign, step)
        block = full.at[weights, place, z, :, columns]
        if axis == 1:
            block = full.at[weights, y, place, :, columns]
        return remote(block, block, first_sem.at[axis * 2 + sign, part, step], along[axis][sign])

    def spread(axis, place):
        for weight in range(2):
            for sign in range(2):
                stream = axis * 2 + sign
                columns = span_of(weight, stream, stream + 1)
                block = full.at[weight, place, z, :, columns]
                if axis == 1:
                    block = full.at[weight, y, place, :, columns]
                sems = second_sem.at[weight, stream, 0]
                remote(block, block, sems, along[1 - axis][sign]).start()

    def second_copy(piece, stream, step):
        weight = min(piece, 2)
        columns = span_of(weight, stream, stream + 1)
        if piece >= 2:
            size = columns.size // 2
            columns = pl.ds(columns.start + (piece - 2) * size, size)
        axis, sign = 1 - stream // 2, stream % 2
        place = place_of(axis, sign, step)
        block = full.at[weight, place, :, :, columns]
        if axis == 1:
            block = full.at[weight, :, place, :, columns]
        return remote(block, block, second_sem.at[piece, stream, step], along[axis][sign])

    for part in range(2):
        for axis in range(2):
            for sign in range(2):
                first_copy(axis, sign, part, 0).start()
    for axis in range(2):
        spread(axis, (y, z)[axis])
    for step in range(1, peers):
        part_copy(step).start()
    for step in range(1, max(HOPS[0]) + 1):
        for axis in range(2):
            for sign in range(2):
                if step <= HOPS[axis][sign]:
                    for part in range(2):
                        first_copy(axis, sign, part, step - 1).wait_recv()
                        if step < HOPS[axis][sign]:
                            first_copy(axis, sign, part, step).start()
                    spread(axis, place_of(axis, sign, step))

    page_copy(pages - 1).start()

    def second_step(pieces, step):
        for piece in pieces:
            for stream in range(STREAMS):
                second_copy(piece, stream, step - 1).wait_recv()
                second_copy(piece, stream, step).start()

    second_step((0, 1), 1)
    page_copy(pages - 2).start()

    for step in range(1, peers):
        part_copy(step).wait_recv()
    for index in (3, 4):
        swaps[index].wait_recv()
    for index in (3, 4, 5):
        locals_[index].wait()
    lines = 32

    def norm_step(step, carry):
        which = step // (tok_count // lines)
        start = pl.multiple_of(lax.rem(step, tok_count // lines) * lines, lines)
        span = pl.ds(start, lines)
        total = both[which, span, :].astype(F32)
        for place in range(tp_count):
            total = total + parts[place * CORES + which, span, :].astype(F32)
        residual[which, span, :] = total
        inverse = lax.rsqrt(jnp.mean(total * total, axis=1, keepdims=True) + 1e-05)
        normed[which, span, :] = (total * inverse * gain_ref[...]).astype(BF16)
        return carry

    lax.fori_loop(0, CORES * tok_count // lines, norm_step, 0)

    def gate_up_step(step, carry):
        second_step((0, 1), step)
        page_copy(pages - 1 - step).start()
        return carry

    lax.fori_loop(2, LAST, gate_up_step, 0)
    for piece in (2, 3):
        for stream in range(STREAMS):
            second_copy(piece, stream, 0).start()
    for piece in (0, 1):
        for stream in range(STREAMS):
            second_copy(piece, stream, LAST - 1).wait_recv()

    chunk = half // RING
    hidden = 128
    all_rows = CORES * tok_count

    def expert_part(index):
        columns = pl.ds(pl.multiple_of(index * chunk, chunk), chunk)
        lhs = normed[...].reshape(all_rows, width)
        pre_gate = jnp.dot(
            lhs, full[0, :, :, :, columns].reshape(width, chunk), preferred_element_type=F32
        )
        pre_up = jnp.dot(
            lhs, full[1, :, :, :, columns].reshape(width, chunk), preferred_element_type=F32
        )
        value = pre_gate / (1.0 + jnp.exp(-pre_gate)) * pre_up
        table = factors[...].reshape(all_rows, 128)
        lanes = lax.broadcasted_iota(jnp.int32, table.shape, 1)
        for expert in range(chunk // hidden):
            picked = jnp.where(lanes == index * (chunk // hidden) + expert, table, 0.0)
            weight = jnp.sum(picked, axis=1, keepdims=True)
            scaled = value[:, expert * hidden : (expert + 1) * hidden] * weight
            spot = pl.ds(pl.multiple_of(index * chunk + expert * hidden, hidden), hidden)
            active[:, spot] = scaled.astype(BF16)

    expert_part(0)

    def down_step(step, carry):
        second_step((2, 3), step)
        expert_part(step)
        return carry

    lax.fori_loop(1, LAST, down_step, 0)
    expert_part(LAST)
    for piece in (2, 3):
        for stream in range(STREAMS):
            second_copy(piece, stream, LAST - 1).wait_recv()

    def back_copy(place, which):
        index = place * CORES + which
        step = lax.rem(index + peers - mine, peers)
        return remote(
            outbox.at[place, which],
            inbox.at[mine],
            back_sem.at[step],
            (chip + which, place),
        )

    height = RING // tp_count

    def down_part(place):
        block = full[2, pl.ds(place * height, height)].reshape(share, half)
        return lax.dot_general(
            active[...], block, (((1,), (1,)), ((), ())), preferred_element_type=F32
        )

    def down_turn(step, carry):
        place = lax.rem(tp + step, tp_count)
        value = down_part(place)
        outbox[place] = value.astype(BF16).reshape(CORES, tok_count, share)
        return carry

    for step in range(1, tp_count):
        down_turn(step, 0)
        if step > 1:
            place = lax.rem(tp + step - 1, tp_count)
            for which in range(CORES):
                back_copy(place, which).start()
    down_turn(0, 0)
    place = lax.rem(tp + tp_count - 1, tp_count)
    for which in range(CORES):
        back_copy(place, which).start()
    back_copy(tp, other).start()

    columns = pl.ds(pl.multiple_of(tp * share, share), share)
    total = residual[core, :, columns] + outbox[tp, core].astype(F32)

    def came(step):
        return remote(outbox.at[tp, other], inbox.at[mine], back_sem.at[step], partner)

    for step in range(1, peers):
        came(step).wait_recv()
        source = lax.rem(mine + peers - step, peers)
        total = total + inbox[source].astype(F32)
    out_ref[...] = total.astype(out_ref.dtype)

    for step in range(1, peers):
        came(step).wait_send()
        part_copy(step).wait_send()
    for copy in swaps:
        copy.wait_send()
    locals_[6].wait()
    for step in range(1, pages):
        page_copy(step).wait()

    for axis in range(2):
        for sign in range(2):
            for step in range(HOPS[axis][sign]):
                for part in range(2):
                    first_copy(axis, sign, part, step).wait_send()

    def drain(step, carry):
        for stream in range(STREAMS):
            for piece in range(4):
                second_copy(piece, stream, step).wait_send()
        return carry

    lax.fori_loop(0, LAST, drain, 0)


def on_device(
    tokens,
    attn_heads,
    out_proj,
    norm_gain,
    w_gate,
    w_up,
    w_down,
    routes,
    gate_weights,
    cache_pages,
    page_dest,
):
    req_count = lax.axis_size("req")
    tp_count = lax.axis_size("tp")
    tok_count, top_count = routes.shape
    experts, rows, hidden = w_gate.shape
    width = tokens.shape[1]
    half = experts * hidden // CORES

    def flat(weight):
        return jnp.transpose(weight, (1, 0, 2)).reshape(rows, experts * hidden)

    part = jnp.dot(attn_heads, out_proj, preferred_element_type=F32).astype(BF16)

    lanes = jnp.arange(128, dtype=jnp.int32)
    own = experts // CORES
    ids = jnp.stack([jnp.where(lanes < own, lanes + h * own, -1) for h in range(CORES)])
    factor = jnp.zeros((CORES, tok_count, 128), F32)
    for route in range(top_count):
        factor = factor + jnp.where(
            routes[None, :, route, None] == ids[:, None, :], gate_weights[None, :, route, None], 0.0
        )

    spread = cache_pages.shape[0]
    places = jnp.arange(spread, dtype=jnp.int32)
    page_order = jnp.sum(
        jnp.where((page_dest % spread)[None, :] == places[:, None], places[None, :], 0), axis=1
    )
    ranked = cache_pages[page_order]

    vmem = pl.BlockSpec(memory_space=pltpu.VMEM)
    anywhere = pl.BlockSpec(memory_space=pl.ANY)
    peers = tp_count * CORES
    share = width // tp_count
    dma = pltpu.SemaphoreType.DMA
    return pl.pallas_call(
        functools.partial(expert_kernel, req_count, tp_count),
        out_shape=(
            jax.ShapeDtypeStruct((tok_count, share), BF16),
            jax.ShapeDtypeStruct(cache_pages.shape, BF16),
        ),
        in_specs=[vmem] * 7 + [anywhere],
        out_specs=(vmem, anywhere),
        scratch_shapes=[
            pltpu.VMEM((3, RING, RING, CORES * rows, half), BF16),
            pltpu.VMEM((peers, tok_count, width), BF16),
            pltpu.VMEM((CORES, tok_count, width), BF16),
            pltpu.VMEM((CORES, tok_count, 128), F32),
            pltpu.VMEM((CORES, tok_count, width), BF16),
            pltpu.VMEM((CORES, tok_count, width), F32),
            pltpu.VMEM((CORES * tok_count, half), BF16),
            pltpu.VMEM((tp_count, CORES, tok_count, share), BF16),
            pltpu.VMEM((peers, tok_count, share), BF16),
            dma((7,)),
            dma((5, 2)),
            dma((peers, 2)),
            dma((spread, 2)),
            dma((STREAMS, 2, max(HOPS[0]), 2)),
            dma((4, STREAMS, LAST, 2)),
            dma((peers, 2)),
        ],
        compiler_params=pltpu.CompilerParams(
            collective_id=0, has_side_effects=True, vmem_limit_bytes=48 * 1024 * 1024
        ),
    )(part, tokens, factor, norm_gain[None, :], flat(w_gate), flat(w_up), flat(w_down), ranked)


def solution(mesh):
    in_specs = (
        P("req", None),
        P("req", "tp"),
        P("tp", None),
        P(),
        P(None, "req", "tp"),
        P(None, "req", "tp"),
        P(None, "req", "tp"),
        P("req", None),
        P("req", None),
        P("req", None, "tp", None),
        P("req"),
    )
    out_specs = (P("req", "tp"), P("req", None, "tp", None))
    return jax.shard_map(
        on_device, mesh=mesh, in_specs=in_specs, out_specs=out_specs, check_vma=False
    )
```

```python
import functools

import jax
import jax.numpy as jnp
from jax import lax
from jax.experimental import pallas as pl
from jax.experimental.pallas import tpu as pltpu
from jax.sharding import PartitionSpec as P

MESH = pl.DeviceIdType.MESH
RING = 8
CORES = 2
STREAMS = 4
LAST = RING - 1
HOPS = ((4, 3), (3, 4))
TILES = ((2, 5, 5, 4), (3, 4, 4, 5), (4, 4, 4, 4))
F32 = jnp.float32
BF16 = jnp.bfloat16


def expert_kernel(
    req_count,
    tp_count,
    part_ref,
    tokens_ref,
    routes_ref,
    weights_ref,
    gain_ref,
    gate_ref,
    up_ref,
    down_ref,
    pages_ref,
    out_ref,
    cache_ref,
    full,
    parts,
    both,
    named,
    shares,
    factors,
    normed,
    residual,
    active,
    outbox,
    inbox,
    local_sem,
    swap_sem,
    part_sem,
    page_sem,
    first_sem,
    second_sem,
    back_sem,
):
    peers = tp_count * CORES
    me = lax.axis_index("req")
    tp = lax.axis_index("tp")
    core = lax.rem(me, CORES)
    z = lax.rem(me // CORES, RING)
    y = me // (CORES * RING)
    mine = tp * CORES + core
    other = 1 - core
    chip = me - core
    tok_count, width = tokens_ref.shape
    half = full.shape[4]
    pages = pages_ref.shape[0]
    share = width // tp_count

    def at(y_place, z_place, core_place):
        return (y_place * RING + z_place) * CORES + core_place

    def peer(index):
        return (chip + lax.rem(index, CORES), index // CORES)

    ahead_y = (at(lax.rem(y + 1, RING), z, core), tp)
    behind_y = (at(lax.rem(y + LAST, RING), z, core), tp)
    ahead_z = (at(y, lax.rem(z + 1, RING), core), tp)
    behind_z = (at(y, lax.rem(z + LAST, RING), core), tp)
    partner = (chip + other, tp)

    barrier = pltpu.get_barrier_semaphore()

    def greet(device):
        pl.semaphore_signal(barrier, inc=1, device_id=device, device_id_type=MESH)

    for device in (ahead_y, behind_y, ahead_z, behind_z):
        greet(device)
    for step in range(1, peers):
        greet(peer(lax.rem(mine + step, peers)))
    for step in range(1, pages):
        greet((lax.rem(me + step, req_count), tp))
        greet((lax.rem(me + req_count - step, req_count), tp))
    pl.semaphore_wait(barrier, 4 + peers - 1 + 2 * (pages - 1))

    def remote(source, target, sems, device):
        return pltpu.make_async_remote_copy(
            src_ref=source,
            dst_ref=target,
            send_sem=sems.at[0],
            recv_sem=sems.at[1],
            device_id=device,
            device_id_type=MESH,
        )

    rows = pl.ds(pl.multiple_of(core * 8, 8), 8)
    kept = pl.ds(pl.multiple_of(core * half, half), half)
    given = pl.ds(pl.multiple_of(other * half, half), half)
    swaps, locals_ = [], []
    for index, weight in enumerate((gate_ref, up_ref, down_ref)):
        place = full.at[index, y, z, rows, :]
        swaps.append(remote(weight.at[:, given], place, swap_sem.at[index], partner))
        locals_.append(pltpu.make_async_copy(weight.at[:, kept], place, local_sem.at[index]))
    swaps.append(remote(tokens_ref, both.at[core], swap_sem.at[3], partner))
    swaps.append(remote(routes_ref, named.at[core], swap_sem.at[4], partner))
    swaps.append(remote(weights_ref, shares.at[core], swap_sem.at[5], partner))
    locals_.append(pltpu.make_async_copy(tokens_ref, both.at[core], local_sem.at[3]))
    locals_.append(pltpu.make_async_copy(routes_ref, named.at[core], local_sem.at[4]))
    locals_.append(pltpu.make_async_copy(weights_ref, shares.at[core], local_sem.at[5]))
    locals_.append(pltpu.make_async_copy(part_ref, parts.at[mine], local_sem.at[6]))
    locals_.append(pltpu.make_async_copy(pages_ref.at[0], cache_ref.at[0], local_sem.at[7]))
    for copy in swaps + locals_:
        copy.start()

    def page_copy(step):
        device = (lax.rem(me + step, req_count), tp)
        return remote(pages_ref.at[step], cache_ref.at[step], page_sem.at[step], device)

    def part_copy(step):
        device = peer(lax.rem(mine + step, peers))
        return remote(part_ref, parts.at[mine], part_sem.at[step], device)

    for index in range(3):
        swaps[index].wait_recv()
        locals_[index].wait()

    def back(place, step):
        return lax.rem(place + RING - step, RING)

    def forth(place, step):
        return lax.rem(place + step, RING)

    def span_of(weight, first, last):
        start = sum(TILES[weight][:first]) * 128
        return pl.ds(start, sum(TILES[weight][first:last]) * 128)

    along = ((ahead_y, behind_y), (ahead_z, behind_z))

    def place_of(axis, sign, step):
        return (back, forth)[sign]((y, z)[axis], step)

    def first_copy(axis, sign, part, step):
        weights = (pl.ds(0, 2), pl.ds(2, 1))[part]
        columns = span_of(2 * part, 2 * axis, 2 * axis + 2)
        place = place_of(axis, sign, step)
        block = full.at[weights, place, z, :, columns]
        if axis == 1:
            block = full.at[weights, y, place, :, columns]
        return remote(block, block, first_sem.at[axis * 2 + sign, part, step], along[axis][sign])

    def spread(axis, place):
        for weight in range(2):
            for sign in range(2):
                stream = axis * 2 + sign
                columns = span_of(weight, stream, stream + 1)
                block = full.at[weight, place, z, :, columns]
                if axis == 1:
                    block = full.at[weight, y, place, :, columns]
                sems = second_sem.at[weight, stream, 0]
                remote(block, block, sems, along[1 - axis][sign]).start()

    def second_copy(piece, stream, step):
        weight = min(piece, 2)
        columns = span_of(weight, stream, stream + 1)
        if piece >= 2:
            size = columns.size // 256 * 128
            if piece == 2:
                columns = pl.ds(columns.start, size)
            else:
                columns = pl.ds(columns.start + size, columns.size - size)
        axis, sign = 1 - stream // 2, stream % 2
        place = place_of(axis, sign, step)
        block = full.at[weight, place, :, :, columns]
        if axis == 1:
            block = full.at[weight, :, place, :, columns]
        return remote(block, block, second_sem.at[piece, stream, step], along[axis][sign])

    for part in range(2):
        for axis in range(2):
            for sign in range(2):
                first_copy(axis, sign, part, 0).start()
    for axis in range(2):
        spread(axis, (y, z)[axis])
    for step in range(1, peers):
        part_copy(step).start()
    turns = [(axis, sign) for axis in range(2) for sign in range(2)]
    for step in range(1, max(HOPS[0]) + 1):
        here = [turn for turn in turns if step <= HOPS[turn[0]][turn[1]]]
        for part in range(2):
            for axis, sign in here:
                first_copy(axis, sign, part, step - 1).wait_recv()
                if step < HOPS[axis][sign]:
                    first_copy(axis, sign, part, step).start()
            if part == 0:
                for axis, sign in here:
                    spread(axis, place_of(axis, sign, step))

    page_copy(pages - 1).start()

    def second_step(pieces, step):
        for piece in pieces:
            for stream in range(STREAMS):
                second_copy(piece, stream, step - 1).wait_recv()
                second_copy(piece, stream, step).start()

    second_step((0, 1), 1)
    page_copy(pages - 2).start()

    for step in range(1, peers):
        part_copy(step).wait_recv()
    for index in (3, 4, 5):
        swaps[index].wait_recv()
    for index in (3, 4, 5, 6):
        locals_[index].wait()
    lines = 32

    own = half // 128
    ids = lax.broadcasted_iota(jnp.int32, (128, tok_count), 0)
    ids = jnp.where(ids < own, ids + core * own, -1)
    for which in range(CORES):
        table = jnp.zeros((128, tok_count), F32)
        for route in range(named.shape[1]):
            hit = named[which, route : route + 1, :] == ids
            table = table + jnp.where(hit, shares[which, route : route + 1, :], 0.0)
        factors[which] = table.T

    def norm_step(step, carry):
        which = step // (tok_count // lines)
        start = pl.multiple_of(lax.rem(step, tok_count // lines) * lines, lines)
        span = pl.ds(start, lines)
        total = both[which, span, :].astype(F32)
        for place in range(tp_count):
            total = total + parts[place * CORES + which, span, :].astype(F32)
        residual[which, span, :] = total
        inverse = lax.rsqrt(jnp.mean(total * total, axis=1, keepdims=True) + 1e-05)
        normed[which, span, :] = (total * inverse * gain_ref[...]).astype(BF16)
        return carry

    lax.fori_loop(0, CORES * tok_count // lines, norm_step, 0)

    def gate_up_step(step, carry):
        second_step((0, 1), step)
        page_copy(pages - 1 - step).start()
        return carry

    lax.fori_loop(2, LAST, gate_up_step, 0)
    for piece in (2, 3):
        for stream in range(STREAMS):
            second_copy(piece, stream, 0).start()
    for piece in (0, 1):
        for stream in range(STREAMS):
            second_copy(piece, stream, LAST - 1).wait_recv()

    chunk = half // RING
    hidden = 128
    all_rows = CORES * tok_count

    def expert_part(index):
        columns = pl.ds(pl.multiple_of(index * chunk, chunk), chunk)
        lhs = normed[...].reshape(all_rows, width)
        pre_gate = jnp.dot(
            lhs, full[0, :, :, :, columns].reshape(width, chunk), preferred_element_type=F32
        )
        pre_up = jnp.dot(
            lhs, full[1, :, :, :, columns].reshape(width, chunk), preferred_element_type=F32
        )
        value = pre_gate / (1.0 + jnp.exp(-pre_gate)) * pre_up
        table = factors[...].reshape(all_rows, 128)
        lanes = lax.broadcasted_iota(jnp.int32, table.shape, 1)
        for expert in range(chunk // hidden):
            picked = jnp.where(lanes == index * (chunk // hidden) + expert, table, 0.0)
            weight = jnp.sum(picked, axis=1, keepdims=True)
            scaled = value[:, expert * hidden : (expert + 1) * hidden] * weight
            spot = pl.ds(pl.multiple_of(index * chunk + expert * hidden, hidden), hidden)
            active[:, spot] = scaled.astype(BF16)

    expert_part(0)

    def down_step(step, carry):
        second_step((2, 3), step)
        expert_part(step)
        return carry

    lax.fori_loop(1, LAST, down_step, 0)
    expert_part(LAST)
    for piece in (2, 3):
        for stream in range(STREAMS):
            second_copy(piece, stream, LAST - 1).wait_recv()

    def back_copy(place, which):
        index = place * CORES + which
        step = lax.rem(index + peers - mine, peers)
        return remote(
            outbox.at[place, which],
            inbox.at[mine],
            back_sem.at[step],
            (chip + which, place),
        )

    height = RING // tp_count

    def down_part(place):
        block = full[2, pl.ds(place * height, height)].reshape(share, half)
        return lax.dot_general(
            active[...], block, (((1,), (1,)), ((), ())), preferred_element_type=F32
        )

    def down_turn(step, carry):
        place = lax.rem(tp + step, tp_count)
        value = down_part(place)
        outbox[place] = value.astype(BF16).reshape(CORES, tok_count, share)
        return carry

    for step in range(1, tp_count):
        down_turn(step, 0)
        if step > 1:
            place = lax.rem(tp + step - 1, tp_count)
            for which in range(CORES):
                back_copy(place, which).start()
    down_turn(0, 0)
    place = lax.rem(tp + tp_count - 1, tp_count)
    for which in range(CORES):
        back_copy(place, which).start()
    back_copy(tp, other).start()

    columns = pl.ds(pl.multiple_of(tp * share, share), share)
    total = residual[core, :, columns] + outbox[tp, core].astype(F32)

    def came(step):
        return remote(outbox.at[tp, other], inbox.at[mine], back_sem.at[step], partner)

    for step in range(1, peers):
        came(step).wait_recv()
        source = lax.rem(mine + peers - step, peers)
        total = total + inbox[source].astype(F32)
    out_ref[...] = total.astype(out_ref.dtype)

    for step in range(1, peers):
        came(step).wait_send()
        part_copy(step).wait_send()
    for copy in swaps:
        copy.wait_send()
    locals_[7].wait()
    for step in range(1, pages):
        page_copy(step).wait()

    for axis in range(2):
        for sign in range(2):
            for step in range(HOPS[axis][sign]):
                for part in range(2):
                    first_copy(axis, sign, part, step).wait_send()

    def drain(step, carry):
        for stream in range(STREAMS):
            for piece in range(4):
                second_copy(piece, stream, step).wait_send()
        return carry

    lax.fori_loop(0, LAST, drain, 0)


def on_device(
    tokens,
    attn_heads,
    out_proj,
    norm_gain,
    w_gate,
    w_up,
    w_down,
    routes,
    gate_weights,
    cache_pages,
    page_dest,
):
    req_count = lax.axis_size("req")
    tp_count = lax.axis_size("tp")
    tok_count, top_count = routes.shape
    experts, rows, hidden = w_gate.shape
    width = tokens.shape[1]
    half = experts * hidden // CORES

    def flat(weight):
        return jnp.transpose(weight, (1, 0, 2)).reshape(rows, experts * hidden)

    part = jnp.dot(attn_heads, out_proj, preferred_element_type=F32).astype(BF16)

    spread = cache_pages.shape[0]
    places = jnp.arange(spread, dtype=jnp.int32)
    page_order = jnp.sum(
        jnp.where((page_dest % spread)[None, :] == places[:, None], places[None, :], 0), axis=1
    )
    ranked = cache_pages[page_order]

    vmem = pl.BlockSpec(memory_space=pltpu.VMEM)
    anywhere = pl.BlockSpec(memory_space=pl.ANY)
    peers = tp_count * CORES
    share = width // tp_count
    dma = pltpu.SemaphoreType.DMA
    return pl.pallas_call(
        functools.partial(expert_kernel, req_count, tp_count),
        out_shape=(
            jax.ShapeDtypeStruct((tok_count, share), BF16),
            jax.ShapeDtypeStruct(cache_pages.shape, BF16),
        ),
        in_specs=[vmem] * 8 + [anywhere],
        out_specs=(vmem, anywhere),
        scratch_shapes=[
            pltpu.VMEM((3, RING, RING, CORES * rows, half), BF16),
            pltpu.VMEM((peers, tok_count, width), BF16),
            pltpu.VMEM((CORES, tok_count, width), BF16),
            pltpu.VMEM((CORES, top_count, tok_count), jnp.int32),
            pltpu.VMEM((CORES, top_count, tok_count), F32),
            pltpu.VMEM((CORES, tok_count, 128), F32),
            pltpu.VMEM((CORES, tok_count, width), BF16),
            pltpu.VMEM((CORES, tok_count, width), F32),
            pltpu.VMEM((CORES * tok_count, half), BF16),
            pltpu.VMEM((tp_count, CORES, tok_count, share), BF16),
            pltpu.VMEM((peers, tok_count, share), BF16),
            dma((8,)),
            dma((6, 2)),
            dma((peers, 2)),
            dma((spread, 2)),
            dma((STREAMS, 2, max(HOPS[0]), 2)),
            dma((4, STREAMS, LAST, 2)),
            dma((peers, 2)),
        ],
        compiler_params=pltpu.CompilerParams(
            collective_id=0, has_side_effects=True, vmem_limit_bytes=48 * 1024 * 1024
        ),
    )(part, tokens, routes.T, gate_weights.T, norm_gain[None, :], flat(w_gate), flat(w_up), flat(w_down), ranked)


def solution(mesh):
    in_specs = (
        P("req", None),
        P("req", "tp"),
        P("tp", None),
        P(),
        P(None, "req", "tp"),
        P(None, "req", "tp"),
        P(None, "req", "tp"),
        P("req", None),
        P("req", None),
        P("req", None, "tp", None),
        P("req"),
    )
    out_specs = (P("req", "tp"), P("req", None, "tp", None))
    return jax.shard_map(
        on_device, mesh=mesh, in_specs=in_specs, out_specs=out_specs, check_vma=False
    )
```

```python
import functools

import jax
import jax.numpy as jnp
from jax import lax
from jax.experimental import pallas as pl
from jax.experimental.pallas import tpu as pltpu
from jax.sharding import PartitionSpec as P

MESH = pl.DeviceIdType.MESH
RING = 8
CORES = 2
STREAMS = 4
LAST = RING - 1
HOPS = ((4, 3), (3, 4))
TILES = ((2, 5, 5, 4), (3, 4, 4, 5), (4, 4, 4, 4))
F32 = jnp.float32
BF16 = jnp.bfloat16


def expert_kernel(
    req_count,
    tp_count,
    part_ref,
    tokens_ref,
    routes_ref,
    weights_ref,
    gain_ref,
    gate_ref,
    up_ref,
    down_ref,
    pages_ref,
    out_ref,
    cache_ref,
    full,
    parts,
    both,
    named,
    shares,
    factors,
    normed,
    residual,
    active,
    outbox,
    inbox,
    local_sem,
    swap_sem,
    part_sem,
    page_sem,
    first_sem,
    second_sem,
    back_sem,
):
    peers = tp_count * CORES
    me = lax.axis_index("req")
    tp = lax.axis_index("tp")
    core = lax.rem(me, CORES)
    z = lax.rem(me // CORES, RING)
    y = me // (CORES * RING)
    mine = tp * CORES + core
    other = 1 - core
    chip = me - core
    tok_count, width = tokens_ref.shape
    half = full.shape[4]
    pages = pages_ref.shape[0]
    share = width // tp_count

    def at(y_place, z_place, core_place):
        return (y_place * RING + z_place) * CORES + core_place

    def peer(index):
        return (chip + lax.rem(index, CORES), index // CORES)

    ahead_y = (at(lax.rem(y + 1, RING), z, core), tp)
    behind_y = (at(lax.rem(y + LAST, RING), z, core), tp)
    ahead_z = (at(y, lax.rem(z + 1, RING), core), tp)
    behind_z = (at(y, lax.rem(z + LAST, RING), core), tp)
    partner = (chip + other, tp)

    barrier = pltpu.get_barrier_semaphore()

    def greet(device):
        pl.semaphore_signal(barrier, inc=1, device_id=device, device_id_type=MESH)

    for device in (ahead_y, behind_y, ahead_z, behind_z):
        greet(device)
    for step in range(1, peers):
        greet(peer(lax.rem(mine + step, peers)))
    for step in range(1, pages):
        greet((lax.rem(me + step, req_count), tp))
        greet((lax.rem(me + req_count - step, req_count), tp))
    pl.semaphore_wait(barrier, 4 + peers - 1 + 2 * (pages - 1))

    def remote(source, target, sems, device):
        return pltpu.make_async_remote_copy(
            src_ref=source,
            dst_ref=target,
            send_sem=sems.at[0],
            recv_sem=sems.at[1],
            device_id=device,
            device_id_type=MESH,
        )

    rows = pl.ds(pl.multiple_of(core * 8, 8), 8)
    kept = pl.ds(pl.multiple_of(core * half, half), half)
    given = pl.ds(pl.multiple_of(other * half, half), half)
    swaps, locals_ = [], []
    for index, weight in enumerate((gate_ref, up_ref, down_ref)):
        place = full.at[index, y, z, rows, :]
        swaps.append(remote(weight.at[:, given], place, swap_sem.at[index], partner))
        locals_.append(pltpu.make_async_copy(weight.at[:, kept], place, local_sem.at[index]))
    swaps.append(remote(tokens_ref, both.at[core], swap_sem.at[3], partner))
    swaps.append(remote(routes_ref, named.at[core], swap_sem.at[4], partner))
    swaps.append(remote(weights_ref, shares.at[core], swap_sem.at[5], partner))
    locals_.append(pltpu.make_async_copy(tokens_ref, both.at[core], local_sem.at[3]))
    locals_.append(pltpu.make_async_copy(routes_ref, named.at[core], local_sem.at[4]))
    locals_.append(pltpu.make_async_copy(weights_ref, shares.at[core], local_sem.at[5]))
    locals_.append(pltpu.make_async_copy(part_ref, parts.at[mine], local_sem.at[6]))
    locals_.append(pltpu.make_async_copy(pages_ref.at[0], cache_ref.at[0], local_sem.at[7]))
    for copy in swaps + locals_:
        copy.start()

    def page_copy(step):
        device = (lax.rem(me + step, req_count), tp)
        return remote(pages_ref.at[step], cache_ref.at[step], page_sem.at[step], device)

    def part_copy(step):
        device = peer(lax.rem(mine + step, peers))
        return remote(part_ref, parts.at[mine], part_sem.at[step], device)

    for index in range(3):
        swaps[index].wait_recv()
        locals_[index].wait()

    def back(place, step):
        return lax.rem(place + RING - step, RING)

    def forth(place, step):
        return lax.rem(place + step, RING)

    def span_of(weight, first, last):
        start = sum(TILES[weight][:first]) * 128
        return pl.ds(start, sum(TILES[weight][first:last]) * 128)

    along = ((ahead_y, behind_y), (ahead_z, behind_z))

    def place_of(axis, sign, step):
        return (back, forth)[sign]((y, z)[axis], step)

    def first_copy(axis, sign, part, step):
        weights = (pl.ds(0, 2), pl.ds(2, 1))[part]
        columns = span_of(2 * part, 2 * axis, 2 * axis + 2)
        place = place_of(axis, sign, step)
        block = full.at[weights, place, z, :, columns]
        if axis == 1:
            block = full.at[weights, y, place, :, columns]
        return remote(block, block, first_sem.at[axis * 2 + sign, part, step], along[axis][sign])

    def spread(axis, place):
        for weight in range(2):
            for sign in range(2):
                stream = axis * 2 + sign
                columns = span_of(weight, stream, stream + 1)
                block = full.at[weight, place, z, :, columns]
                if axis == 1:
                    block = full.at[weight, y, place, :, columns]
                sems = second_sem.at[weight, stream, 0]
                remote(block, block, sems, along[1 - axis][sign]).start()

    def second_copy(piece, stream, step):
        weight = min(piece, 2)
        columns = span_of(weight, stream, stream + 1)
        if piece >= 2:
            size = columns.size // 256 * 128
            if piece == 2:
                columns = pl.ds(columns.start, size)
            else:
                columns = pl.ds(columns.start + size, columns.size - size)
        axis, sign = 1 - stream // 2, stream % 2
        place = place_of(axis, sign, step)
        block = full.at[weight, place, :, :, columns]
        if axis == 1:
            block = full.at[weight, :, place, :, columns]
        return remote(block, block, second_sem.at[piece, stream, step], along[axis][sign])

    for part in range(2):
        for axis in range(2):
            for sign in range(2):
                first_copy(axis, sign, part, 0).start()
    for axis in range(2):
        spread(axis, (y, z)[axis])
    for step in range(1, peers):
        part_copy(step).start()
    turns = [(axis, sign) for axis in range(2) for sign in range(2)]
    for step in range(1, max(HOPS[0]) + 1):
        here = [turn for turn in turns if step <= HOPS[turn[0]][turn[1]]]
        for part in range(2):
            for axis, sign in here:
                first_copy(axis, sign, part, step - 1).wait_recv()
                if step < HOPS[axis][sign]:
                    first_copy(axis, sign, part, step).start()
            if part == 0:
                for axis, sign in here:
                    spread(axis, place_of(axis, sign, step))

    page_copy(pages - 1).start()

    def second_step(pieces, step):
        for streams in ((1, 2, 3), (0,)):
            for piece in pieces:
                for stream in streams:
                    second_copy(piece, stream, step - 1).wait_recv()
                    second_copy(piece, stream, step).start()

    second_step((0, 1), 1)
    page_copy(pages - 2).start()

    for step in range(1, peers):
        part_copy(step).wait_recv()
    for index in (3, 4, 5):
        swaps[index].wait_recv()
    for index in (3, 4, 5, 6):
        locals_[index].wait()
    lines = 32

    own = half // 128
    ids = lax.broadcasted_iota(jnp.int32, (128, tok_count), 0)
    ids = jnp.where(ids < own, ids + core * own, -1)
    for which in range(CORES):
        table = jnp.zeros((128, tok_count), F32)
        for route in range(named.shape[1]):
            hit = named[which, route : route + 1, :] == ids
            table = table + jnp.where(hit, shares[which, route : route + 1, :], 0.0)
        factors[which] = table.T

    def norm_step(step, carry):
        which = step // (tok_count // lines)
        start = pl.multiple_of(lax.rem(step, tok_count // lines) * lines, lines)
        span = pl.ds(start, lines)
        total = both[which, span, :].astype(F32)
        for place in range(tp_count):
            total = total + parts[place * CORES + which, span, :].astype(F32)
        residual[which, span, :] = total
        inverse = lax.rsqrt(jnp.mean(total * total, axis=1, keepdims=True) + 1e-05)
        normed[which, span, :] = (total * inverse * gain_ref[...]).astype(BF16)
        return carry

    lax.fori_loop(0, CORES * tok_count // lines, norm_step, 0)

    def gate_up_step(step, carry):
        second_step((0, 1), step)
        page_copy(pages - 1 - step).start()
        return carry

    lax.fori_loop(2, LAST, gate_up_step, 0)
    for piece in (2, 3):
        for stream in range(STREAMS):
            second_copy(piece, stream, 0).start()
    for piece in (0, 1):
        for stream in range(STREAMS):
            second_copy(piece, stream, LAST - 1).wait_recv()

    chunk = half // RING
    hidden = 128
    all_rows = CORES * tok_count

    def expert_part(index):
        columns = pl.ds(pl.multiple_of(index * chunk, chunk), chunk)
        lhs = normed[...].reshape(all_rows, width)
        pre_gate = jnp.dot(
            lhs, full[0, :, :, :, columns].reshape(width, chunk), preferred_element_type=F32
        )
        pre_up = jnp.dot(
            lhs, full[1, :, :, :, columns].reshape(width, chunk), preferred_element_type=F32
        )
        value = pre_gate / (1.0 + jnp.exp(-pre_gate)) * pre_up
        table = factors[...].reshape(all_rows, 128)
        lanes = lax.broadcasted_iota(jnp.int32, table.shape, 1)
        for expert in range(chunk // hidden):
            picked = jnp.where(lanes == index * (chunk // hidden) + expert, table, 0.0)
            weight = jnp.sum(picked, axis=1, keepdims=True)
            scaled = value[:, expert * hidden : (expert + 1) * hidden] * weight
            spot = pl.ds(pl.multiple_of(index * chunk + expert * hidden, hidden), hidden)
            active[:, spot] = scaled.astype(BF16)

    expert_part(0)

    def down_step(step, carry):
        second_step((2, 3), step)
        expert_part(step)
        return carry

    lax.fori_loop(1, LAST, down_step, 0)
    expert_part(LAST)
    for piece in (2, 3):
        for stream in range(STREAMS):
            second_copy(piece, stream, LAST - 1).wait_recv()

    def back_copy(place, which):
        index = place * CORES + which
        step = lax.rem(index + peers - mine, peers)
        return remote(
            outbox.at[place, which],
            inbox.at[mine],
            back_sem.at[step],
            (chip + which, place),
        )

    height = RING // tp_count

    def down_part(place):
        block = full[2, pl.ds(place * height, height)].reshape(share, half)
        return lax.dot_general(
            active[...], block, (((1,), (1,)), ((), ())), preferred_element_type=F32
        )

    def down_turn(step, carry):
        place = lax.rem(tp + step, tp_count)
        value = down_part(place)
        outbox[place] = value.astype(BF16).reshape(CORES, tok_count, share)
        return carry

    for step in range(1, tp_count):
        down_turn(step, 0)
        if step > 1:
            place = lax.rem(tp + step - 1, tp_count)
            for which in range(CORES):
                back_copy(place, which).start()
    down_turn(0, 0)
    place = lax.rem(tp + tp_count - 1, tp_count)
    for which in range(CORES):
        back_copy(place, which).start()
    back_copy(tp, other).start()

    columns = pl.ds(pl.multiple_of(tp * share, share), share)
    total = residual[core, :, columns] + outbox[tp, core].astype(F32)

    def came(step):
        return remote(outbox.at[tp, other], inbox.at[mine], back_sem.at[step], partner)

    for step in range(1, peers):
        came(step).wait_recv()
        source = lax.rem(mine + peers - step, peers)
        total = total + inbox[source].astype(F32)
    out_ref[...] = total.astype(out_ref.dtype)

    for step in range(1, peers):
        came(step).wait_send()
        part_copy(step).wait_send()
    for copy in swaps:
        copy.wait_send()
    locals_[7].wait()
    for step in range(1, pages):
        page_copy(step).wait()

    for axis in range(2):
        for sign in range(2):
            for step in range(HOPS[axis][sign]):
                for part in range(2):
                    first_copy(axis, sign, part, step).wait_send()

    def drain(step, carry):
        for stream in range(STREAMS):
            for piece in range(4):
                second_copy(piece, stream, step).wait_send()
        return carry

    lax.fori_loop(0, LAST, drain, 0)


def on_device(
    tokens,
    attn_heads,
    out_proj,
    norm_gain,
    w_gate,
    w_up,
    w_down,
    routes,
    gate_weights,
    cache_pages,
    page_dest,
):
    req_count = lax.axis_size("req")
    tp_count = lax.axis_size("tp")
    tok_count, top_count = routes.shape
    experts, rows, hidden = w_gate.shape
    width = tokens.shape[1]
    half = experts * hidden // CORES

    def flat(weight):
        return jnp.transpose(weight, (1, 0, 2)).reshape(rows, experts * hidden)

    part = jnp.dot(attn_heads, out_proj, preferred_element_type=F32).astype(BF16)

    spread = cache_pages.shape[0]
    places = jnp.arange(spread, dtype=jnp.int32)
    page_order = jnp.sum(
        jnp.where((page_dest % spread)[None, :] == places[:, None], places[None, :], 0), axis=1
    )
    ranked = cache_pages[page_order]

    vmem = pl.BlockSpec(memory_space=pltpu.VMEM)
    anywhere = pl.BlockSpec(memory_space=pl.ANY)
    peers = tp_count * CORES
    share = width // tp_count
    dma = pltpu.SemaphoreType.DMA
    return pl.pallas_call(
        functools.partial(expert_kernel, req_count, tp_count),
        out_shape=(
            jax.ShapeDtypeStruct((tok_count, share), BF16),
            jax.ShapeDtypeStruct(cache_pages.shape, BF16),
        ),
        in_specs=[vmem] * 8 + [anywhere],
        out_specs=(vmem, anywhere),
        scratch_shapes=[
            pltpu.VMEM((3, RING, RING, CORES * rows, half), BF16),
            pltpu.VMEM((peers, tok_count, width), BF16),
            pltpu.VMEM((CORES, tok_count, width), BF16),
            pltpu.VMEM((CORES, top_count, tok_count), jnp.int32),
            pltpu.VMEM((CORES, top_count, tok_count), F32),
            pltpu.VMEM((CORES, tok_count, 128), F32),
            pltpu.VMEM((CORES, tok_count, width), BF16),
            pltpu.VMEM((CORES, tok_count, width), F32),
            pltpu.VMEM((CORES * tok_count, half), BF16),
            pltpu.VMEM((tp_count, CORES, tok_count, share), BF16),
            pltpu.VMEM((peers, tok_count, share), BF16),
            dma((8,)),
            dma((6, 2)),
            dma((peers, 2)),
            dma((spread, 2)),
            dma((STREAMS, 2, max(HOPS[0]), 2)),
            dma((4, STREAMS, LAST, 2)),
            dma((peers, 2)),
        ],
        compiler_params=pltpu.CompilerParams(
            collective_id=0, has_side_effects=True, vmem_limit_bytes=48 * 1024 * 1024
        ),
    )(part, tokens, routes.T, gate_weights.T, norm_gain[None, :], flat(w_gate), flat(w_up), flat(w_down), ranked)


def solution(mesh):
    in_specs = (
        P("req", None),
        P("req", "tp"),
        P("tp", None),
        P(),
        P(None, "req", "tp"),
        P(None, "req", "tp"),
        P(None, "req", "tp"),
        P("req", None),
        P("req", None),
        P("req", None, "tp", None),
        P("req"),
    )
    out_specs = (P("req", "tp"), P("req", None, "tp", None))
    return jax.shard_map(
        on_device, mesh=mesh, in_specs=in_specs, out_specs=out_specs, check_vma=False
    )
```
